32 devices in a mesh: dp: 2 (over core), narrow: 4 (over y, x), wide: 4 (over z).
Axes of the slice: x: 2, y: 2, z: 4, core: 2. Of those that a mesh axis runs over, the one named last changes fastest.
Arguments:
- tokens: bfloat16 [8192, 2048], P(('dp', 'narrow', 'wide')), may hold values from -6 to 6
- document_lengths: int32 [8, 8], P(('dp', 'narrow')), may hold values from 1 to 512, 1024 in all within a row
- attn_gain: bfloat16 [2048], P('narrow'), may hold values from 0.5 to 1.5
- query_projection_weight: bfloat16 [2048, 2048], P('narrow', 'wide'), may hold values from -0.125 to 0.125
- key_projection_weight: bfloat16 [2048, 512], P('narrow'), may hold values from -0.125 to 0.125
- value_projection_weight: bfloat16 [2048, 512], P('narrow'), may hold values from -0.125 to 0.125
- output_weight: bfloat16 [2048, 2048], P('wide', 'narrow'), may hold values from -1 to 1
- mlp_gain: bfloat16 [2048], P('narrow'), may hold values from 0.5 to 1.5
- gate_weight: bfloat16 [2048, 8192], P('narrow', 'wide'), may hold values from -0.125 to 0.125
- up_weight: bfloat16 [2048, 8192], P('narrow', 'wide'), may hold values from -0.125 to 0.125
- down_weight: bfloat16 [8192, 2048], P('wide', 'narrow'), may hold values from -0.0625 to 0.0625
- output_cotangent: bfloat16 [8192, 2048], P(('dp', 'narrow', 'wide')), may hold values from -6 to 6
Outputs:
- layer_out: bfloat16 [8192, 2048], P(('dp', 'narrow', 'wide'))
- tokens_grad: float32 [8192, 2048], P(('dp', 'narrow', 'wide'))
- attn_gain_grad: float32 [2048], P(('dp', 'narrow', 'wide'))
- query_grad: float32 [2048, 2048], P(('dp', 'narrow'), 'wide')
- key_grad: float32 [2048, 512], P(('dp', 'narrow'), 'wide')
- value_grad: float32 [2048, 512], P(('dp', 'narrow'), 'wide')
- output_grad: float32 [2048, 2048], P('wide', ('dp', 'narrow'))
- mlp_gain_grad: float32 [2048], P(('dp', 'narrow', 'wide'))
- gate_grad: float32 [2048, 8192], P(('dp', 'narrow'), 'wide')
- up_grad: float32 [2048, 8192], P(('dp', 'narrow'), 'wide')
- down_grad: float32 [8192, 2048], P('wide', ('dp', 'narrow'))
The draws below stay inside these ranges and needn't reach their ends.
Inputs may be any that keep to these rules, and one draw needn't show every extreme that they name: `document_lengths`: in every row the 8 lengths are 1 or more and sum to 1024, and the longest is exactly 512.
All inputs are finite; a program needn't handle non-finite values.
Results may differ from the reference program's by a relative error of at most 0.025.
Values may be sent and summed in bfloat16 or wider, within the bound.
No kernel may reach another device: no remote copies, remote signals or barrier semaphores. Data moves between devices by JAX's collectives and lax.ppermute only.
A program may use at most 320 MiB of HBM per device.

```python
import math
import jax
import jax.numpy as jnp
import numpy as np
from jax import lax

MODEL_WIDTH = 2048
QUERY_HEADS = 32
KEY_VALUE_HEADS = 8
HEAD_SIZE = 64
FF = 8192
DOCS_PER_ROW = 8
PACKED_LENGTH = 1024
PACKED_ROWS = 8
TOKENS = 8192
LONGEST_DOC = 512


def level_of(key, dims, shards, smallest, top_value):
    gain = 1.0
    for dim, shards_of in shards:
        steps = jax.random.uniform(jax.random.fold_in(jax.random.fold_in(key, 6), dim), (shards_of,), jnp.float32, smallest / len(shards), top_value / len(shards))
        gain = gain * jnp.repeat(jnp.exp(steps), dims[dim] // shards_of).reshape((-1,) + (1,) * (len(dims) - 1 - dim))
    return gain


def split_up(count, total, bound, slope):
    portions = [(1 << 20) // math.isqrt(grade ** slope) + 1 for grade in range(2, count + 1)]
    rest, counts = total - bound - (count - 1), [1] * (count - 1)
    while rest > 0:
        candidates = [i for i in range(count - 1) if counts[i] < bound]
        mass, budget = sum([portions[i] for i in candidates]), rest
        for i in candidates:
            addition = min(bound - counts[i], max(1, budget * portions[i] // mass), rest)
            counts[i] = counts[i] + addition
            rest = rest - addition
    return np.array([bound] + counts)


def ragged(own_key, count, total, most, skew):
    if count == 2:
        one = jax.random.randint(own_key, (), max(1, total - most), min(most, total - 1) + 1)
        return jnp.stack([one, total - one])
    tallies = jnp.asarray(split_up(count, total, most, skew), jnp.int32)
    twos = (count - 1) // 2
    giver, sink = tallies[1:1 + 2 * twos:2], tallies[2:2 + 2 * twos:2]
    slack = jnp.minimum(giver - 1, most - sink)
    moved = jax.random.randint(jax.random.fold_in(own_key, 1), (twos,), 0, 1 << 20) % (slack + 1)
    tallies = tallies.at[1:1 + 2 * twos:2].set(giver - moved).at[2:2 + 2 * twos:2].set(sink + moved)
    return tallies[jax.random.permutation(jax.random.fold_in(own_key, 2), count)]


def centred(own_key, dims, scale, bound, split=(), kind=jnp.bfloat16):
    values = jax.random.normal(own_key, dims, jnp.float32) * scale
    if len(split) > 0:
        values = level_of(own_key, dims, split, -0.22, 0.18) * values
    return jnp.clip(values, min=-bound, max=bound).astype(kind)


def setup_inputs(seed: int = 0) -> dict:
    key_of = jax.random.split(jax.random.key(seed), 13)
    tokens = centred(key_of[0], (TOKENS, MODEL_WIDTH), 1.0, 6.0, ((0, 32),))
    document_lengths = jax.vmap(lambda own: ragged(own, DOCS_PER_ROW, PACKED_LENGTH, LONGEST_DOC, 2))(jax.random.split(key_of[1], PACKED_ROWS)).reshape((PACKED_ROWS, DOCS_PER_ROW)).astype(jnp.int32)
    attn_gain = jnp.clip(1.0 + 0.1 * jax.random.normal(key_of[2], (MODEL_WIDTH,), jnp.float32), 0.5, 1.5).astype(jnp.bfloat16)
    query_projection_weight = centred(key_of[3], (MODEL_WIDTH, QUERY_HEADS * HEAD_SIZE), MODEL_WIDTH ** -0.5, 0.125, ((0, 4), (1, 4)))
    key_projection_weight = centred(key_of[4], (MODEL_WIDTH, KEY_VALUE_HEADS * HEAD_SIZE), MODEL_WIDTH ** -0.5, 0.125, ((0, 4),))
    value_projection_weight = centred(key_of[5], (MODEL_WIDTH, KEY_VALUE_HEADS * HEAD_SIZE), MODEL_WIDTH ** -0.5, 0.125, ((0, 4),))
    output_weight = centred(key_of[6], (QUERY_HEADS * HEAD_SIZE, MODEL_WIDTH), (QUERY_HEADS * HEAD_SIZE // 64) ** -0.5, 1.0, ((0, 4), (1, 4)))
    mlp_gain = jnp.clip(1.0 + 0.1 * jax.random.normal(key_of[7], (MODEL_WIDTH,), jnp.float32), 0.5, 1.5).astype(jnp.bfloat16)
    gate_weight = centred(key_of[8], (MODEL_WIDTH, FF), MODEL_WIDTH ** -0.5, 0.125, ((0, 4), (1, 4)))
    up_weight = centred(key_of[9], (MODEL_WIDTH, FF), MODEL_WIDTH ** -0.5, 0.125, ((0, 4), (1, 4)))
    down_weight = centred(key_of[10], (FF, MODEL_WIDTH), FF ** -0.5, 0.0625, ((0, 4), (1, 4)))
    output_cotangent = centred(key_of[11], (TOKENS, MODEL_WIDTH), 1.0, 6.0, ((0, 32),))
    return dict(tokens=tokens, document_lengths=document_lengths, attn_gain=attn_gain, query_projection_weight=query_projection_weight, key_projection_weight=key_projection_weight, value_projection_weight=value_projection_weight, output_weight=output_weight, mlp_gain=mlp_gain, gate_weight=gate_weight, up_weight=up_weight, down_weight=down_weight, output_cotangent=output_cotangent)


epsilon = 1e-05

@jax.custom_vjp
def low(v):
    return lax.optimization_barrier(v.astype(jnp.bfloat16)).astype(jnp.float32)

@jax.custom_vjp
def low_back(v):
    return v

def low_keep(v):
    return (low(v), None)

def low_pass(kept, grad):
    return (grad,)

def back_keep(v):
    return (v, None)

def back_low(kept, grad):
    return (low(grad),)
low.defvjp(low_keep, low_pass)
low_back.defvjp(back_keep, back_low)

def highest_precision(left, right):
    return jnp.dot(left, right, precision=lax.Precision.HIGHEST)

def rope_tables(positions, head_dim):
    half_dim = head_dim // 2
    freq_index = jnp.arange(half_dim, dtype=jnp.float32)
    inverse = 500000.0 ** (-2.0 * freq_index / head_dim)
    wavelength = 2.0 * math.pi / inverse
    smooth_part = (8192.0 / wavelength - 1.0) / 3.0
    blended = (1.0 - smooth_part) * inverse / 32.0 + smooth_part * inverse
    scaled = jnp.where(wavelength < 2048.0, inverse, jnp.where(wavelength > 8192.0, inverse / 32.0, blended))
    angles = positions.astype(jnp.float32)[:, None] * scaled[None, :]
    cosine = jnp.cos(angles)
    sine_table = jnp.sin(angles)
    return (jnp.concatenate([cosine, cosine], 1), jnp.concatenate([sine_table, sine_table], 1))

def rotate(value_rows_matrix, cosine, sine_table):
    half_dim = value_rows_matrix.shape[-1] // 2
    turned = jnp.concatenate([-value_rows_matrix[..., half_dim:], value_rows_matrix[..., :half_dim]], -1)
    return value_rows_matrix * cosine[:, None, :] + turned * sine_table[:, None, :]

def row_layout(row_lengths):
    ends = jnp.cumsum(row_lengths).astype(jnp.int32)
    starts = (ends - row_lengths).astype(jnp.int32)
    token_positions_list = jnp.arange(PACKED_LENGTH, dtype=jnp.int32)
    segment = lax.optimization_barrier(jnp.sum((token_positions_list[:, None] >= ends[None, :]).astype(jnp.int32), 1)).astype(jnp.int32)
    chosen = segment[:, None] == jnp.arange(DOCS_PER_ROW, dtype=jnp.int32)[None, :]
    position = (token_positions_list - lax.optimization_barrier(jnp.sum(jnp.where(chosen, starts[None, :], 0), 1))).astype(jnp.int32)
    return (segment, position)

def attend(query_rows_matrix, key_row_matrix, value_rows_matrix, segment):
    group_size = QUERY_HEADS // KEY_VALUE_HEADS
    keys_wide = jnp.repeat(key_row_matrix, group_size, axis=1)
    values_wide = jnp.repeat(value_rows_matrix, group_size, axis=1)
    row_block_list = min(512, PACKED_LENGTH)
    block_list = PACKED_LENGTH // row_block_list
    token_positions_list = jnp.arange(PACKED_LENGTH, dtype=jnp.int32)
    query_blocks = query_rows_matrix.reshape(block_list, row_block_list, QUERY_HEADS, HEAD_SIZE)
    segment_blocks = segment.reshape(block_list, row_block_list)
    place_blocks = token_positions_list.reshape(block_list, row_block_list)

    def one_block(block_inputs):
        query_part, segment_part, place_part = block_inputs
        scores = jnp.einsum('qhd,khd->hqk', query_part, keys_wide, precision=lax.Precision.HIGHEST) * (1.0 / math.sqrt(HEAD_SIZE))
        scores = low_back(scores)
        visible = (segment_part[:, None] == segment[None, :]) & (place_part[:, None] >= token_positions_list[None, :])
        scores = jnp.where(visible[None], scores, -1e+30)
        largest = lax.optimization_barrier(jnp.max(scores, -1, keepdims=True))
        weights = jnp.exp(scores - largest)
        weights = weights / lax.optimization_barrier(jnp.sum(weights, -1, keepdims=True))
        return jnp.einsum('hqk,khd->qhd', low(weights), values_wide, precision=lax.Precision.HIGHEST)
    layer_outputs = lax.map(jax.checkpoint(one_block), (query_blocks, segment_blocks, place_blocks))
    return layer_outputs.reshape(PACKED_LENGTH, QUERY_HEADS * HEAD_SIZE)

def layer_row(weights, row_tokens, segment, position):
    attn_gain, query_projection_weight, key_projection_weight, value_projection_weight, output_weight, mlp_gain, gate_weight, up_weight, down_weight = weights
    cosine, sine_table = rope_tables(position, HEAD_SIZE)
    inv_first = lax.rsqrt(lax.optimization_barrier(jnp.mean(row_tokens * row_tokens, -1, keepdims=True)) + epsilon)
    normed_input = low(row_tokens * inv_first * attn_gain)
    query_rows_matrix = low_back(highest_precision(normed_input, query_projection_weight)).reshape(PACKED_LENGTH, QUERY_HEADS, HEAD_SIZE)
    key_row_matrix = low_back(highest_precision(normed_input, key_projection_weight)).reshape(PACKED_LENGTH, KEY_VALUE_HEADS, HEAD_SIZE)
    value_rows_matrix = low(low_back(highest_precision(normed_input, value_projection_weight))).reshape(PACKED_LENGTH, KEY_VALUE_HEADS, HEAD_SIZE)
    query_rows_matrix = low(rotate(query_rows_matrix, cosine, sine_table))
    key_row_matrix = low(rotate(key_row_matrix, cosine, sine_table))
    attended = attend(query_rows_matrix, key_row_matrix, value_rows_matrix, segment)
    branch = low_back(highest_precision(low(low_back(attended)), output_weight))
    hidden = row_tokens + branch
    inv_second = lax.rsqrt(lax.optimization_barrier(jnp.mean(hidden * hidden, -1, keepdims=True)) + epsilon)
    normed_mlp = low(hidden * inv_second * mlp_gain)
    gate_value = low_back(highest_precision(normed_mlp, gate_weight))
    up_value = low_back(highest_precision(normed_mlp, up_weight))
    activated = low(jax.nn.silu(gate_value) * up_value)
    return hidden + low_back(highest_precision(activated, down_weight))

def reference(tokens, document_lengths, attn_gain, query_projection_weight, key_projection_weight, value_projection_weight, output_weight, mlp_gain, gate_weight, up_weight, down_weight, output_cotangent):
    params = (attn_gain.astype(jnp.float32), query_projection_weight.astype(jnp.float32), key_projection_weight.astype(jnp.float32), value_projection_weight.astype(jnp.float32), output_weight.astype(jnp.float32), mlp_gain.astype(jnp.float32), gate_weight.astype(jnp.float32), up_weight.astype(jnp.float32), down_weight.astype(jnp.float32))
    packed_input_rows = tokens.astype(jnp.float32).reshape(PACKED_ROWS, PACKED_LENGTH, MODEL_WIDTH)
    segments, positions = jax.vmap(row_layout)(document_lengths)

    def forward(weights, inputs):

        def step(carried, row_inputs):
            row_tokens, segment, position = row_inputs
            return (carried, jax.checkpoint(layer_row)(weights, row_tokens, segment, position))
        ignored, layer_outputs = lax.scan(step, jnp.zeros((), jnp.float32), (inputs, segments, positions))
        return layer_outputs
    layer_outputs, backward_function = jax.vjp(forward, params, packed_input_rows)
    parameter_gradients, row_input_gradient = backward_function(output_cotangent.astype(jnp.float32).reshape(PACKED_ROWS, PACKED_LENGTH, MODEL_WIDTH))
    return (layer_outputs.reshape(TOKENS, MODEL_WIDTH).astype(jnp.bfloat16), row_input_gradient.reshape(TOKENS, MODEL_WIDTH), parameter_gradients[0], parameter_gradients[1], parameter_gradients[2], parameter_gradients[3], parameter_gradients[4], parameter_gradients[5], parameter_gradients[6], parameter_gradients[7], parameter_gradients[8])
```

```python
import functools
import math

import jax
import jax.numpy as jnp
from jax import lax
from jax.experimental import pallas as pl
from jax.experimental.pallas import tpu as pltpu
from jax.sharding import PartitionSpec as P

QUERY_HEADS = 32
KEY_VALUE_HEADS = 8
HEAD_SIZE = 64
LANES = 128

epsilon = 1e-05
masked_score = -1e30
f32 = jnp.float32
bf16 = jnp.bfloat16

ROWS_BY_COLS = (((1,), (0,)), ((), ()))
BOTH_LAST = (((1,), (1,)), ((), ()))
BOTH_FIRST = (((0,), (0,)), ((), ()))
brief = pl.CostEstimate(flops=1024, bytes_accessed=1024, transcendentals=0)


def mm(left, right, dims=ROWS_BY_COLS):
    return lax.dot_general(left, right, dims, preferred_element_type=f32)


def after(value, *earlier):
    return lax.optimization_barrier((value, *earlier))[0]


def fence(*values):
    leaves, tree = jax.tree.flatten(values)
    return jax.tree.unflatten(tree, lax.optimization_barrier(leaves))


def rope_tables(positions, head_dim):
    half_dim = head_dim // 2
    lane = jnp.arange(LANES, dtype=jnp.int32)
    freq_index = (lane % half_dim).astype(f32)
    inverse = 500000.0 ** (-2.0 * freq_index / head_dim)
    wavelength = 2.0 * math.pi / inverse
    smooth_part = (8192.0 / wavelength - 1.0) / 3.0
    blended = (1.0 - smooth_part) * inverse / 32.0 + smooth_part * inverse
    scaled = jnp.where(
        wavelength < 2048.0, inverse, jnp.where(wavelength > 8192.0, inverse / 32.0, blended)
    )
    angles = positions.astype(f32)[:, None] * scaled[None, :]
    sign = jnp.where(lane % head_dim < half_dim, -1.0, 1.0)
    return jnp.cos(angles), jnp.sin(angles) * sign[None, :]


def swap_halves(u, first_half):
    return jnp.where(first_half, pltpu.roll(u, LANES - 32, 1), pltpu.roll(u, 32, 1))


def attention_forward_kernel(
    blocks, pairs, info, proj, cos, sin, start, qs, k2, v2, att, att_low, lse
):
    rows_of = proj.shape[0] // blocks
    own = info[0]
    nq = pairs * LANES
    lane = lax.broadcasted_iota(jnp.int32, (rows_of, LANES), 1)
    low = lane < HEAD_SIZE
    first_half = lane % HEAD_SIZE < HEAD_SIZE // 2

    def prepare(r, carry):
        rows = pl.ds(pl.multiple_of(r * rows_of, rows_of), rows_of)
        c, s = cos[rows, :], sin[rows, :]

        def rotate(u):
            return u * c + swap_halves(u, first_half) * s

        for p in range(pairs):
            u = proj[rows, p * LANES : (p + 1) * LANES]
            qs[rows, p * LANES : (p + 1) * LANES] = (rotate(u) * 0.125).astype(bf16)
        u = proj[rows, nq : nq + LANES]
        turned = pltpu.roll(u, HEAD_SIZE, 1)
        k2[rows, :] = rotate(jnp.where(low, u, turned)).astype(bf16)
        v2[rows, :] = jnp.where(low, turned, u).astype(bf16)
        return carry

    lax.fori_loop(0, blocks, prepare, 0)

    def block(r, carry):
        s = lax.rem(own - r + blocks, blocks)
        rows = pl.ds(pl.multiple_of(r * rows_of, rows_of), rows_of)
        begin = start[rows, :]
        place = s * rows_of + lax.broadcasted_iota(jnp.int32, (rows_of, 1), 0)
        totals = jnp.zeros((rows_of, LANES), f32)
        for p in range(pairs):
            q = qs[rows, p * LANES : (p + 1) * LANES]
            zero = jnp.zeros_like(q)
            halves = (jnp.where(low, q, zero), jnp.where(low, zero, q))

            def step(kb, state, halves=halves):
                kr = lax.rem(own - kb + blocks, blocks)
                krows = pl.ds(pl.multiple_of(kr * rows_of, rows_of), rows_of)
                kc, vc = k2[krows, :], v2[krows, :]
                key = kb * rows_of + lax.broadcasted_iota(jnp.int32, (rows_of, rows_of), 1)
                visible = (key >= begin) & (key <= place)
                new = []
                for qh, (m, l, acc) in zip(halves, state):
                    scores = jnp.where(visible, mm(qh, kc, BOTH_LAST), masked_score)
                    m_new = jnp.maximum(m, jnp.max(scores, -1, keepdims=True))
                    weights = jnp.exp(scores - m_new)
                    scale = jnp.exp(m - m_new)
                    l = scale * l + jnp.sum(weights, -1, keepdims=True)
                    acc = scale * acc + mm(weights.astype(bf16), vc)
                    new.append((m_new, l, acc))
                return tuple(new)

            empty = (
                jnp.full((rows_of, 1), masked_score, f32),
                jnp.zeros((rows_of, 1), f32),
                jnp.zeros((rows_of, LANES), f32),
            )
            (m0, l0, acc0), (m1, l1, acc1) = lax.fori_loop(
                info[1 + s], s + 1, step, (empty, empty)
            )
            out = jnp.where(low, acc0 / l0, acc1 / l1)
            att[rows, p * LANES : (p + 1) * LANES] = out
            att_low[rows, p * LANES : (p + 1) * LANES] = out.astype(bf16)
            totals = jnp.where(lane == 2 * p, m0 + jnp.log(l0), totals)
            totals = jnp.where(lane == 2 * p + 1, m1 + jnp.log(l1), totals)
        lse[rows, :] = totals
        return carry

    lax.fori_loop(0, blocks, block, 0)


def attention_backward_kernel(
    blocks, pairs, info, qs, k2, v2, grad, att, lse, cos, sin, start, *refs
):
    out, dk, dv = refs[-3:]
    rows_of = qs.shape[0] // blocks
    own = info[0]
    nq = pairs * LANES
    lane = lax.broadcasted_iota(jnp.int32, (rows_of, LANES), 1)
    low = lane < HEAD_SIZE
    first_half = lane % HEAD_SIZE < HEAD_SIZE // 2
    dk[...] = jnp.zeros_like(dk)
    dv[...] = jnp.zeros_like(dv)

    def block(r, carry):
        s = lax.rem(own - r + blocks, blocks)
        rows = pl.ds(pl.multiple_of(r * rows_of, rows_of), rows_of)
        begin = start[rows, :]
        place = s * rows_of + lax.broadcasted_iota(jnp.int32, (rows_of, 1), 0)
        totals = lse[rows, :]
        c, sn = cos[rows, :], sin[rows, :]
        for p in range(pairs):
            cols = slice(p * LANES, (p + 1) * LANES)
            q, d = qs[rows, cols], grad[rows, cols]
            zero = jnp.zeros_like(q)
            product = d.astype(f32) * att[rows, cols]
            heads = []
            for h in range(2):
                mine = low if h == 0 else jnp.logical_not(low)
                heads.append(
                    (
                        jnp.where(mine, q, zero),
                        jnp.where(mine, d, zero),
                        jnp.sum(jnp.where(mine, product, 0.0), -1, keepdims=True),
                        jnp.sum(jnp.where(lane == 2 * p + h, totals, 0.0), -1, keepdims=True),
                    )
                )

            def step(kb, state, heads=heads):
                kr = lax.rem(own - kb + blocks, blocks)
                krows = pl.ds(pl.multiple_of(kr * rows_of, rows_of), rows_of)
                kc, vc = k2[krows, :], v2[krows, :]
                key = kb * rows_of + lax.broadcasted_iota(jnp.int32, (rows_of, rows_of), 1)
                visible = (key >= begin) & (key <= place)
                new, dk_add, dv_add = [], None, None
                for (qh, dh, dot, total), dq in zip(heads, state):
                    scores = mm(qh, kc, BOTH_LAST) - total
                    weights = jnp.exp(jnp.where(visible, scores, masked_score))
                    weight_grad = mm(dh, vc, BOTH_LAST)
                    score_low = (weights * (weight_grad - dot)).astype(bf16)
                    new.append(dq + mm(score_low, kc))
                    dk_part = mm(score_low, qh, BOTH_FIRST)
                    dv_part = mm(weights.astype(bf16), dh, BOTH_FIRST)
                    dk_add = dk_part if dk_add is None else dk_add + dk_part
                    dv_add = dv_part if dv_add is None else dv_add + dv_part
                dk[krows, :] += dk_add
                dv[krows, :] += dv_add
                return tuple(new)

            nothing = jnp.zeros((rows_of, LANES), f32)
            dq0, dq1 = lax.fori_loop(info[1 + s], s + 1, step, (nothing, nothing))
            dq = jnp.where(low, dq0, dq1) * 0.125
            out[rows, cols] = (dq * c + swap_halves(dq * sn, first_half)).astype(bf16)
        return carry

    lax.fori_loop(0, blocks, block, 0)

    def finish(r, carry):
        rows = pl.ds(pl.multiple_of(r * rows_of, rows_of), rows_of)

        def total(ref):
            u = ref[rows, :]
            return u + pltpu.roll(u, HEAD_SIZE, 1)

        u = total(dk)
        u = u * cos[rows, :] + swap_halves(u * sin[rows, :], first_half)
        out[rows, nq : nq + LANES] = jnp.where(low, u, total(dv)).astype(bf16)
        return carry

    lax.fori_loop(0, blocks, finish, 0)


def in_vmem(count):
    return [pl.BlockSpec(memory_space=pltpu.VMEM)] * count


def attention_forward(info, proj, cos, sin, start, blocks):
    length = proj.shape[0]
    nq = proj.shape[1] - LANES
    pairs = nq // LANES
    shapes = (
        jax.ShapeDtypeStruct((length, nq), bf16),
        jax.ShapeDtypeStruct((length, LANES), bf16),
        jax.ShapeDtypeStruct((length, LANES), bf16),
        jax.ShapeDtypeStruct((length, nq), f32),
        jax.ShapeDtypeStruct((length, nq), bf16),
        jax.ShapeDtypeStruct((length, LANES), f32),
    )
    return pl.pallas_call(
        functools.partial(attention_forward_kernel, blocks, pairs),
        out_shape=shapes,
        in_specs=[pl.BlockSpec(memory_space=pltpu.SMEM)] + in_vmem(4),
        out_specs=tuple(in_vmem(6)),
        cost_estimate=brief,
        name="attention_forward",
    )(info, proj, cos, sin, start)


def attention_backward(info, splits, saved, grad, cos, sin, start, blocks, kept):
    qs, k2, v2, att, _, lse = saved
    length, nq = qs.shape
    pairs = nq // LANES
    cols = nq + LANES
    args = [info, qs, k2, v2, grad, att, lse, cos, sin, start]
    in_specs = [pl.BlockSpec(x.shape, lambda i, info: (0, 0)) for x in args[1:]]
    aliases = {}
    if kept is not None:
        aliases = {len(args): 0}
        args.append(kept)
        in_specs.append(pl.BlockSpec(memory_space=pl.ANY))
    return pl.pallas_call(
        functools.partial(attention_backward_kernel, blocks, pairs),
        out_shape=jax.ShapeDtypeStruct((length, splits * cols), bf16),
        grid_spec=pltpu.PrefetchScalarGridSpec(
            num_scalar_prefetch=1,
            grid=(1,),
            in_specs=in_specs,
            out_specs=pl.BlockSpec((length, cols), lambda i, info: (0, info[1 + blocks])),
            scratch_shapes=[pltpu.VMEM((length, LANES), f32)] * 2,
        ),
        input_output_aliases=aliases,
        cost_estimate=brief,
        name="attention_backward",
    )(*args)


def absolute_tile(step, core, tiles):
    half = step // tiles
    return (half + core[0] - 2 * half * core[0]) * tiles + step % tiles


def feed_forward_kernel(tiles, core, x, grad, gm, um, dm, go, uo, do, *refs):
    x_all, grad_all, act, gate_up_low, back, out, back_sum, out_sum = refs[-8:]
    tile = act.shape[1]
    i = pl.program_id(0)

    @pl.when(i == 0)
    def _():
        back_sum[...] = jnp.zeros_like(back_sum)
        out_sum[...] = jnp.zeros_like(out_sum)
        x_all[...] = x[...]
        grad_all[...] = grad[...]

    def run(gate_w, up_w, down_w):
        rows = x[...]
        gate_value = mm(rows, gate_w[...])
        up_value = mm(rows, up_w[...])
        act_grad = mm(grad[...], down_w[...], BOTH_LAST)
        sigmoid_gate = jax.nn.sigmoid(gate_value)
        silu_gate = gate_value * sigmoid_gate
        a = (silu_gate * up_value).astype(bf16)
        g = (
            act_grad * up_value * (sigmoid_gate * (1.0 + gate_value * (1.0 - sigmoid_gate)))
        ).astype(bf16)
        u = (act_grad * silu_gate).astype(bf16)
        act[...] = a
        at = pl.multiple_of(absolute_tile(i, core, tiles) * tile, tile)
        gate_up_low[:, pl.ds(at, tile)] = g
        at = pl.multiple_of(at + 2 * tiles * tile, tile)
        gate_up_low[:, pl.ds(at, tile)] = u
        back_sum[...] += mm(g, gate_w[...], BOTH_LAST) + mm(u, up_w[...], BOTH_LAST)
        out_sum[...] += mm(a, down_w[...])

    @pl.when(i < tiles)
    def _():
        run(gm, um, dm)

    @pl.when(i >= tiles)
    def _():
        run(go, uo, do)

    @pl.when(i == 2 * tiles - 1)
    def _():
        back[...] = back_sum[...].astype(bf16)
        out[...] = out_sum[...].astype(bf16)


def feed_forward(part, parts, core, x, grad, own, other, kept):
    rows, width = x.shape
    units = own[1].shape[0]
    tile = min(256, units)
    tiles = units // tile
    first = lambda i: jnp.minimum(i, tiles - 1)
    second = lambda i: jnp.maximum(i - tiles, 0)
    whole = pl.BlockSpec((rows, width), lambda i, c: (0, 0))

    def weights(at):
        return [
            pl.BlockSpec((width, tile), lambda i, c: (0, at(i))),
            pl.BlockSpec((width, tile), lambda i, c: (0, tiles + at(i))),
            pl.BlockSpec((tile, width), lambda i, c: (at(i), 0)),
        ]

    columns = (width, width, 2 * units, 4 * units)
    kept_shapes = tuple(jax.ShapeDtypeStruct((rows * parts, k), bf16) for k in columns)
    kept_specs = (
        pl.BlockSpec((rows, width), lambda i, c: (part, 0)),
        pl.BlockSpec((rows, width), lambda i, c: (part, 0)),
        pl.BlockSpec((rows, tile), lambda i, c: (part, absolute_tile(i, c, tiles))),
        pl.BlockSpec((rows, 4 * units), lambda i, c: (part, 0)),
    )
    args = [core[None], x, grad, own[0], own[0], own[1], other[0], other[0], other[1]]
    in_specs = [whole, whole] + weights(first) + weights(second)
    aliases = {}
    if kept is not None:
        aliases = {len(args) + k: k for k in range(4)}
        args += kept
        in_specs += [pl.BlockSpec(memory_space=pl.ANY)] * 4
    result = pl.pallas_call(
        functools.partial(feed_forward_kernel, tiles),
        out_shape=kept_shapes + (jax.ShapeDtypeStruct((rows, width), bf16),) * 2,
        grid_spec=pltpu.PrefetchScalarGridSpec(
            num_scalar_prefetch=1,
            grid=(2 * tiles,),
            in_specs=in_specs,
            out_specs=kept_specs + (whole,) * 2,
            scratch_shapes=[pltpu.VMEM((rows, width), f32)] * 2,
        ),
        input_output_aliases=aliases,
        cost_estimate=brief,
        name="feed_forward",
    )(*args)
    return list(result[:4]), result[4], result[5]


def on_device(
    tokens,
    document_lengths,
    attn_gain,
    query_projection_weight,
    key_projection_weight,
    value_projection_weight,
    output_weight,
    mlp_gain,
    gate_weight,
    up_weight,
    down_weight,
    output_cotangent,
):
    wide = lax.axis_size("wide")
    narrow = lax.axis_size("narrow")
    cores = lax.axis_size("dp")
    wide_index = lax.axis_index("wide")
    narrow_index = lax.axis_index("narrow")
    core = lax.axis_index("dp")
    other = 1 - core
    local_heads = query_projection_weight.shape[1] // HEAD_SIZE
    group_size = QUERY_HEADS // KEY_VALUE_HEADS
    local_kv = max(1, local_heads // group_size)
    kv_first = wide_index * local_heads // group_size
    nq = local_heads * HEAD_SIZE
    nkv = local_kv * HEAD_SIZE
    own_rows, width = tokens.shape
    length = own_rows * wide
    pairs = local_heads // 2
    half_width = width // 2

    def shift(x, by):
        return lax.ppermute(x, "wide", [(i, (i + by) % wide) for i in range(wide)])

    def swap(x):
        return lax.ppermute(x, "dp", [(i, 1 - i) for i in range(cores)])

    def across(x, bits):
        return lax.ppermute(x, "narrow", [(i, i ^ bits) for i in range(narrow)])

    def ring_reduce(part):
        total = part(1 % wide)
        for k in range(2, wide + 1):
            come = shift(total, 1)
            total = come.astype(f32) + part(k % wide).astype(f32)
            if k < wide:
                total = total.astype(bf16)
        return total

    def narrow_near(x):
        return across(x, 1), across(x, 2)

    def narrow_far(by_x, by_y):
        mid = by_x.shape[0] // 2
        return across(by_x[:mid], 2), across(by_y[mid:], 1)

    def narrow_place(x, near, far, axis):
        rows, cols = x.shape
        size, mid = x.shape[axis], rows // 2
        full = jnp.zeros((rows * narrow, cols) if axis == 0 else (rows, cols * narrow), x.dtype)
        pieces = ((0, x, 0), (1, near[0], 0), (2, near[1], 0), (3, far[0], 0), (3, far[1], mid))
        for bits, piece, row in pieces:
            at = (narrow_index ^ bits) * size
            full = lax.dynamic_update_slice(full, piece, (at + row, 0) if axis == 0 else (row, at))
        return full

    def narrow_scatter(x, axis):
        size = x.shape[axis] // narrow
        cut = x.shape[1 - axis] // 2

        def piece(bits, which):
            begin = [0, 0]
            begin[axis] = (narrow_index ^ bits) * size
            begin[1 - axis] = which * cut
            shape = [cut, cut]
            shape[axis] = size
            return lax.dynamic_slice(x, begin, shape)

        far_b = across(piece(3, 1), 1)
        far_a = across(piece(3, 0), 2)
        x_b = across(piece(1, 1), 1)
        y_a = across(piece(2, 0), 2)
        x_a = across((piece(1, 0).astype(f32) + far_a.astype(f32)).astype(bf16), 1)
        y_b = across((piece(2, 1).astype(f32) + far_b.astype(f32)).astype(bf16), 2)
        first = piece(0, 0).astype(f32) + x_a.astype(f32) + y_a.astype(f32)
        second = piece(0, 1).astype(f32) + x_b.astype(f32) + y_b.astype(f32)
        return first, second

    def sum_all(x):
        x = x + swap(x)
        for axis, size in (("narrow", narrow), ("wide", wide)):
            bits = 1
            while bits < size:
                x = x + lax.ppermute(x, axis, [(i, i ^ bits) for i in range(size)])
                bits *= 2
        return x

    def half(x, which, axis):
        size = x.shape[axis] // 2
        return lax.dynamic_slice_in_dim(x, which * size, size, axis)

    def in_place(x, axis):
        return jnp.where(core == 0, x, exchanged(x, axis))

    def exchanged(x, axis):
        size = x.shape[axis] // 2
        a, b = lax.slice_in_dim(x, 0, size, axis=axis), lax.slice_in_dim(x, size, 2 * size, axis=axis)
        return jnp.concatenate([b, a], axis)

    lengths = document_lengths[0]
    docs = lengths.shape[0]
    upto = jnp.arange(docs)[:, None] <= jnp.arange(docs)[None, :]
    ends = jnp.sum(jnp.where(upto, lengths[:, None], 0), 0)
    starts = ends - lengths

    def start_of(place):
        segment = jnp.sum((place[:, None] >= ends[None, :]).astype(jnp.int32), 1)
        chosen = segment[:, None] == jnp.arange(docs, dtype=jnp.int32)[None, :]
        return jnp.sum(jnp.where(chosen, starts[None, :], 0), 1)

    row = jnp.arange(length, dtype=jnp.int32)
    place = (wide_index - row // own_rows + wide) % wide * own_rows + row % own_rows
    start = start_of(place)
    cos, sin = rope_tables(place - start, HEAD_SIZE)
    columns = start[:, None]
    first_keys = start_of(jnp.arange(wide, dtype=jnp.int32) * own_rows) // own_rows
    info = jnp.concatenate([wide_index[None].astype(jnp.int32), first_keys.astype(jnp.int32)])

    splits = 2 if local_kv % 2 == 0 else 1
    part = own_rows
    nq_half = nq // 2
    token_parts = [tokens, shift(tokens, 1)]
    key_own = lax.dynamic_slice_in_dim(key_projection_weight, kv_first * HEAD_SIZE, nkv, 1)
    value_own = lax.dynamic_slice_in_dim(value_projection_weight, kv_first * HEAD_SIZE, nkv, 1)
    head_weights = (query_projection_weight, key_own, value_own)
    if splits == 2:
        head_weights = tuple(half(x, core, 1) for x in head_weights)
    gains = jnp.stack([attn_gain, mlp_gain], 1)
    gains = jnp.pad(gains, ((0, 0), (0, LANES - 2)))
    head_weights = jnp.concatenate((*head_weights, gains), 1)
    near = narrow_near(head_weights)
    gate_up_half = jnp.concatenate([half(gate_weight, core, 1), half(up_weight, core, 1)], 1)
    gate_up_m = lax.all_gather(gate_up_half, "narrow", axis=0, tiled=True)
    output_half = half(output_weight, core, 0)
    down_half = half(down_weight, core, 0)
    token_parts[1], near, cos, sin, columns, info, output_half, down_half = fence(
        token_parts[1], near, cos, sin, columns, info, output_half, down_half
    )

    token_parts.append(shift(token_parts[1], 1))
    far = narrow_far(*near)
    token_parts[2], far = fence(token_parts[2], far)

    for r in range(3, wide):
        token_parts.append(shift(token_parts[-1], 1))
    ready = after(output_half, token_parts[2])
    wo_parts = [output_half] + [shift(ready, r) for r in range(1, wide)]
    wqkv_m = narrow_place(head_weights, near, far, 0)
    gain_rows = mm(jnp.eye(8, LANES, dtype=bf16), wqkv_m[:, -LANES:], BOTH_LAST)
    wqkv_m = wqkv_m[:, :-LANES]
    wqkv = (wqkv_m, swap(wqkv_m))[:splits]
    attn_gain_row, mlp_gain_row = gain_rows[0:1], gain_rows[1:2]
    normed, invs, projected = [], [], []

    def project(x):
        x = x.astype(f32)
        invs.append(lax.rsqrt(jnp.mean(x * x, -1, keepdims=True) + epsilon))
        normed.append((x * invs[-1] * attn_gain_row).astype(bf16))
        projected.append([mm(normed[-1], w) for w in wqkv])

    def unit(r):
        return token_parts[r].astype(f32) * invs[r]

    for r in range(wide - 2):
        project(token_parts[r])
    token_parts[-1], wo_parts, projected, gate_up_m = fence(
        token_parts[-1], wo_parts, projected, gate_up_m
    )

    def attend(h):
        proj = jnp.concatenate([p[h] for p in projected], 0)
        return attention_forward(info, proj, cos, sin, columns, wide)

    def to_rows(att_low):
        return [att_low[:part]] + [
            shift(att_low[r * part : (r + 1) * part], -r) for r in range(1, wide)
        ]

    grad_parts = [output_cotangent, shift(after(output_cotangent, token_parts[-1]), 1)]
    wo_own = jnp.concatenate([wo_parts[-r % wide] for r in range(wide)], 0)
    wo_m = lax.all_gather(wo_own, "narrow", axis=1, tiled=True)
    down_m = lax.all_gather(after(down_half, wo_own), "narrow", axis=1, tiled=True)
    for r in range(wide - 2, wide):
        project(token_parts[r])
    saved = [attend(0)]
    grad_parts[1], saved, projected = fence(grad_parts[1], saved, projected)

    att_own = [to_rows(saved[0][4])]
    gate_up_o = swap(after(gate_up_m, saved[0][4]))
    if splits == 2:
        saved.append(attend(1))
    att_own, saved, gate_up_o = fence(att_own, saved, gate_up_o)

    if splits == 2:
        att_own.append(to_rows(saved[1][4]))
    else:
        att_own = [[half(a, which, 1) for a in att_own[0]] for which in (core, other)]
    wo_o = swap(after(wo_m, saved[-1][4]))
    att_own = [jnp.concatenate(a, 1) for a in att_own]
    att_own, wo_o = fence(att_own, wo_o)

    grad_parts.append(shift(after(grad_parts[-1], att_own[1]), 1))
    inputs = tokens.astype(f32)
    hidden = inputs + (mm(att_own[0], wo_m) + mm(att_own[1], wo_o))
    inv_second = lax.rsqrt(jnp.mean(hidden * hidden, -1, keepdims=True) + epsilon)
    normed_mlp = (hidden * inv_second * mlp_gain_row).astype(bf16)
    grad_parts[2:], hidden, inv_second, normed_mlp = fence(
        grad_parts[2:], hidden, inv_second, normed_mlp
    )
    unit_second = hidden * inv_second
    down_o = swap(after(down_m, normed_mlp))

    mlp_parts, kept, mlp_outs, first_back, reducing = [normed_mlp], None, [], None, None
    for r in range(wide):
        come = []
        if r + 1 < wide:
            come.append(shift(mlp_parts[r], 1))
        if 3 <= r + 2 < wide:
            come.append(shift(grad_parts[r + 1], 1))
        if r == 2 % wide:
            reducing = shift(back, 1)
        elif r > 2:
            total = reducing.astype(f32) + back.astype(f32)
            reducing = shift(total.astype(bf16), 1)
        kept, back, out = feed_forward(
            r, wide, core, mlp_parts[r], grad_parts[r], (gate_up_m, down_m), (gate_up_o, down_o), kept
        )
        mlp_outs.append(out)
        come, back, reducing = fence(come, back, reducing)
        if r + 1 < wide:
            mlp_parts.append(come[0])
        if 3 <= r + 2 < wide:
            grad_parts.append(come[1])
        if r == 0:
            first_back = back
    mlp_all, grad_all, acts, gate_up_lows = kept

    def rows_sent(left, right):
        return mm(half(left, other, 1), right, BOTH_FIRST).astype(bf16)

    def rows_kept(left, right, come):
        return (mm(half(left, core, 1), right, BOTH_FIRST) + come.astype(f32)).astype(bf16)

    def cols_sent(left, right):
        return mm(left, half(right, other, 1), BOTH_FIRST).astype(bf16)

    def cols_kept(left, right, come):
        return (mm(left, half(right, core, 1), BOTH_FIRST) + come.astype(f32)).astype(bf16)

    def narrow_sum(x, axis):
        return lax.psum_scatter(x, "narrow", scatter_dimension=axis, tiled=True)

    total = reducing.astype(f32) + back.astype(f32)
    reducing = shift(total.astype(bf16), 1)
    down_sent = cols_sent(acts, grad_all)
    gate_up_sent = rows_sent(mlp_all, gate_up_lows)
    reducing, down_sent, gate_up_sent = fence(reducing, down_sent, gate_up_sent)

    normed_mlp_grad = reducing.astype(f32) + first_back.astype(f32)
    out_reducing = shift(after(mlp_outs[1 % wide], reducing), 1)
    down_come, gate_up_come = swap(down_sent), swap(gate_up_sent)
    scaled_second = normed_mlp_grad * mlp_gain_row
    mlp_gain_part = jnp.sum(normed_mlp_grad * unit_second, 0)
    hidden_grad = output_cotangent.astype(f32) + inv_second * (
        scaled_second - unit_second * jnp.mean(scaled_second * unit_second, -1, keepdims=True)
    )
    hidden_low = hidden_grad.astype(bf16)
    head_grads = []
    for w in (wo_m, wo_o):
        back = mm(hidden_low, w, BOTH_LAST).astype(bf16)
        head_grads.append([back[:, r * nq_half : (r + 1) * nq_half] for r in range(wide)])
    if splits == 1:
        head_grads = [[jnp.concatenate(pair, 1) for pair in zip(*head_grads)]]
    out_reducing, down_come, gate_up_come, head_grads, hidden_grad, hidden_low, mlp_gain_part = fence(
        out_reducing, down_come, gate_up_come, head_grads, hidden_grad, hidden_low, mlp_gain_part
    )

    def spread(parts):
        return jnp.concatenate([x if r == 0 else shift(x, r) for r, x in enumerate(parts)], 0)

    def attend_back(h, attended_grad, earlier):
        at = jnp.abs(core - h)[None] * (splits - 1)
        return attention_backward(
            jnp.concatenate([info, at.astype(jnp.int32)]),
            splits, saved[h], attended_grad, cos, sin, columns, wide, earlier,
        )

    attended_grad = spread(head_grads[0])
    if splits == 1:
        attended_grad = in_place(attended_grad, 1)
    down_sum = cols_kept(after(acts, hidden_low), grad_all, down_come)
    att_both = in_place(jnp.concatenate([after(x, hidden_low) for x in att_own], 1), 1)
    out_sent = cols_sent(att_both, hidden_low)
    attended_grad, down_sum, att_both, out_sent = fence(attended_grad, down_sum, att_both, out_sent)

    down_grad = narrow_sum(down_sum, 1).astype(f32)
    out_come = swap(out_sent)
    projected_low = attend_back(0, attended_grad, None)
    if splits == 2:
        attended_grad = spread(head_grads[1])
    attended_grad, projected_low, out_come = fence(attended_grad, projected_low, out_come)

    if wide > 2:
        total = (out_reducing.astype(f32) + mlp_outs[2].astype(f32)).astype(bf16)
        out_reducing = shift(after(total, projected_low), 1)
    if splits == 2:
        projected_low = attend_back(1, attended_grad, projected_low)
    out_sum = cols_kept(att_both, after(hidden_low, attended_grad), out_come)
    wqkv_all = wqkv[0] if splits == 1 else jnp.concatenate(wqkv, 1)
    if splits == 2:
        wqkv_all = in_place(after(wqkv_all, attended_grad), 1)
    out_reducing, projected_low, out_sum, wqkv_all = fence(
        out_reducing, projected_low, out_sum, wqkv_all
    )

    out_sum = narrow_sum(out_sum, 1)
    ng_parts = [
        mm(projected_low[r * part : (r + 1) * part], wqkv_all, BOTH_LAST).astype(bf16) for r in range(wide)
    ]
    normed_grad = shift(ng_parts[1 % wide], 1)
    gate_up_sum = rows_kept(mlp_all, after(gate_up_lows, projected_low), gate_up_come)
    attn_gain_part = sum(jnp.sum(g.astype(f32) * unit(r), 0) for r, g in enumerate(ng_parts))
    normed_grad, ng_parts, gate_up_sum, attn_gain_part = fence(
        normed_grad, ng_parts, gate_up_sum, attn_gain_part
    )

    gate_up_sum = narrow_sum(gate_up_sum, 0)
    normed_all = jnp.concatenate([after(x, normed_grad) for x in normed], 0)
    for k in range(2, wide):
        total = (normed_grad.astype(f32) + ng_parts[k].astype(f32)).astype(bf16)
        normed_grad = shift(total, 1)
        if k == 2:
            project_come = swap(rows_sent(normed_all, projected_low))
            project_sum = rows_kept(normed_all, projected_low, project_come)
            gain_sums = sum_all(jnp.stack([attn_gain_part, mlp_gain_part]))
        if k > 2:
            total = out_reducing.astype(f32) + mlp_outs[k].astype(f32)
            out_reducing = shift(total.astype(bf16), 1)
        if k == 2:
            normed_grad, project_sum, gain_sums = fence(normed_grad, project_sum, gain_sums)
    project_grad = jnp.concatenate(narrow_scatter(project_sum, 0), 1)
    normed_grad = normed_grad.astype(f32) + ng_parts[0].astype(f32)
    mlp_branch = out_reducing.astype(f32) + mlp_outs[0].astype(f32)
    layer_out = (hidden + mlp_branch).astype(bf16)
    scaled_first = normed_grad * attn_gain_row
    tokens_grad = hidden_grad + invs[0] * (
        scaled_first - unit(0) * jnp.mean(scaled_first * unit(0), -1, keepdims=True)
    )

    out_m, out_o = jnp.split(out_sum, 2, 0)

    def out_part(r):
        at = r * nq_half
        return jnp.concatenate([out_m[at : at + nq_half], out_o[at : at + nq_half]], 0)

    output_grad = out_part(0).astype(f32)
    for r in range(1, wide):
        output_grad = output_grad + shift(out_part(r), r).astype(f32)
    gate_grad, up_grad = jnp.split(gate_up_sum.astype(f32), 2, 1)

    heads_grad = jnp.split(project_grad, splits, 1)
    nq_part, nkv_part = nq // splits, nkv // splits
    query_grad = jnp.concatenate([g[:, :nq_part] for g in heads_grad], 1)
    key_grad = jnp.concatenate([g[:, nq_part : nq_part + nkv_part] for g in heads_grad], 1)
    value_grad = jnp.concatenate([g[:, nq_part + nkv_part :] for g in heads_grad], 1)
    total_kv = key_projection_weight.shape[1]

    def kv_grad(part):
        if nkv * wide == total_kv:
            return part
        embed = lax.dynamic_update_slice_in_dim(
            jnp.zeros((part.shape[0], total_kv), bf16), part.astype(bf16), kv_first * HEAD_SIZE, 1
        )
        return lax.psum_scatter(embed, "wide", scatter_dimension=1, tiled=True).astype(f32)

    key_grad, value_grad = kv_grad(key_grad), kv_grad(value_grad)

    gain_own = width // (cores * narrow * wide)
    gain_at = ((core * narrow + narrow_index) * wide + wide_index) * gain_own
    gain_sums = lax.dynamic_slice_in_dim(gain_sums, gain_at, gain_own, 1)
    return (
        layer_out,
        tokens_grad,
        gain_sums[0],
        query_grad,
        key_grad,
        value_grad,
        output_grad,
        gain_sums[1],
        gate_grad,
        up_grad,
        down_grad,
    )


def solution(mesh):
    return jax.shard_map(
        on_device,
        mesh=mesh,
        in_specs=(
            P(("dp", "narrow", "wide"), None),
            P(("dp", "narrow"), None),
            P("narrow"),
            P("narrow", "wide"),
            P("narrow", None),
            P("narrow", None),
            P("wide", "narrow"),
            P("narrow"),
            P("narrow", "wide"),
            P("narrow", "wide"),
            P("wide", "narrow"),
            P(("dp", "narrow", "wide"), None),
        ),
        out_specs=(
            P(("dp", "narrow", "wide"), None),
            P(("dp", "narrow", "wide"), None),
            P(("dp", "narrow", "wide")),
            P(("dp", "narrow"), "wide"),
            P(("dp", "narrow"), "wide"),
            P(("dp", "narrow"), "wide"),
            P("wide", ("dp", "narrow")),
            P(("dp", "narrow", "wide")),
            P(("dp", "narrow"), "wide"),
            P(("dp", "narrow"), "wide"),
            P("wide", ("dp", "narrow")),
        ),
        check_vma=False,
    )
```
